32 devices in a mesh: sweep: 2 (over x), cx: 4 (over z), cy: 4 (over y, core).
Axes of the slice: x: 2, y: 2, z: 4, core: 2. Of those that a mesh axis runs over, the one named last changes fastest.
Arguments:
- right_side: float32 [2, 320, 32, 512], P('sweep', None, 'cx', 'cy'), may hold values from -6 to 6
- inverse_table: bfloat16 [4, 320, 320], replicated, may hold values from -1 to 3
- coupling_table: bfloat16 [2, 6, 80, 320], replicated, may hold values from -0.3125 to 0.3125
- block_kind: int32 [2, 32, 512], P('sweep', 'cx', 'cy'), may hold values from 0 to 3
- face_kind: int32 [2, 6, 32, 512], P('sweep', None, 'cx', 'cy'), may hold values from 0 to 1
Outputs:
- solution: float32 [2, 320, 32, 512], P('sweep', None, 'cx', 'cy')
The draws below stay inside these ranges and needn't reach their ends.
All inputs are finite; a program needn't handle non-finite values.
Results may differ from the reference program's by a relative error of at most 0.0095.
Values may be sent and summed in bfloat16 or wider, within the bound.
A program may use at most 64 MiB of HBM per device.

```python
import math
import jax
import jax.numpy as jnp
from jax import lax

NVAR = 5
NP = 4
BLOCK = 320
TRACE = 80
KD = 4
KC = 2
SWEEPS = 2
NS = 2
NX = 32
NY = 512


def draw_inverse_table(key, part):
    first_key, second_key = jax.random.split(key)
    index_row = jnp.arange(BLOCK)
    identity = (index_row[:, None] == index_row[None, :]).astype(jnp.float32)
    diagonal = jax.random.uniform(first_key, (KD, BLOCK, 1), jnp.float32, 0.5, 1.5)
    spread = jax.random.truncated_normal(second_key, -4.0, 4.0, (KD, BLOCK, BLOCK), jnp.float32) * (0.3 / math.sqrt(BLOCK))
    return (identity * diagonal + (1.0 - identity) * spread).astype(jnp.bfloat16)


def with_ends(array, own_key, low, high):
    longest = array.shape.index(max(array.shape))
    spots = []
    for shift in (0, 1):
        where = [jax.random.randint(jax.random.fold_in(own_key, axis), (), 0, length) for axis, length in enumerate(array.shape)]
        where[longest] = (where[longest] + shift) % array.shape[longest]
        spots.append(tuple(where))
    return array.at[spots[0]].set(low).at[spots[1]].set(high)


def steps_of(stream_key, dims, pieces, low, top_value):
    def one(position, blocks):
        draws = jax.random.uniform(jax.random.fold_in(jax.random.fold_in(stream_key, 6), position), (blocks,), jnp.float32, low / len(pieces), top_value / len(pieces))
        return jnp.repeat(jnp.exp(draws), dims[position] // blocks).reshape((-1,) + (1,) * (len(dims) - position - 1))

    factor_of = one(*pieces[0])
    for cut in pieces[1:]:
        factor_of = factor_of * one(*cut)
    return factor_of


def bell_draw(key, extent, width, most, cuts=(), kind=jnp.bfloat16):
    drawn = width * jax.random.normal(key, extent, jnp.float32)
    if cuts:
        drawn = drawn * steps_of(key, extent, cuts, -0.22, 0.18)
    return jnp.clip(drawn, -most, most).astype(kind)


def setup_inputs(seed: int = 0) -> dict:
    key_list = jax.random.split(jax.random.key(seed), 6)
    return {
        "right_side": bell_draw(key_list[0], (NS, BLOCK, NX, NY), 1.0, 6.0, ((0, 2), (2, 4), (3, 4)), jnp.float32),
        "inverse_table": draw_inverse_table(jax.random.fold_in(key_list[5], 71), 0),
        "coupling_table": bell_draw(key_list[2], (KC, 6, TRACE, BLOCK), (4 * TRACE) ** -0.5, 0.3125),
        "block_kind": with_ends(jax.random.randint(key_list[3], (NS, NX, NY), 0, KD), jax.random.fold_in(key_list[3], 1), 0, KD - 1).astype(jnp.int32),
        "face_kind": with_ends(jax.random.randint(key_list[4], (NS, 6, NX, NY), 0, KC), jax.random.fold_in(key_list[4], 1), 0, KC - 1).astype(jnp.int32),
    }


def face_traces(iterate):
    plane_count, _, width_x, width_y = iterate.shape
    node_view = iterate.reshape(plane_count, NVAR, NP, NP, NP, width_x, width_y)
    picked = (node_view[:, :, 0], node_view[:, :, NP - 1], node_view[:, :, :, 0], node_view[:, :, :, NP - 1], node_view[:, :, :, :, 0], node_view[:, :, :, :, NP - 1])
    return [member.reshape(plane_count, TRACE, width_x, width_y).astype(jnp.bfloat16) for member in picked]


def from_below(source, along_dim):
    length = source.shape[along_dim]
    zero_row = jnp.zeros_like(lax.slice_in_dim(source, 0, 1, axis=along_dim))
    return jnp.concatenate([zero_row, lax.slice_in_dim(source, 0, length - 1, axis=along_dim)], axis=along_dim)


def from_above(source, along_dim):
    length = source.shape[along_dim]
    zero_row = jnp.zeros_like(lax.slice_in_dim(source, 0, 1, axis=along_dim))
    return jnp.concatenate([lax.slice_in_dim(source, 1, length, axis=along_dim), zero_row], axis=along_dim)


def couple_terms(incoming, kinds_plane, coupling_table):
    accumulated = jnp.zeros((BLOCK,) + incoming[0].shape[1:], jnp.float32)
    for face_index in range(6):
        for kind_index in range(KC):
            masked = jnp.where(kinds_plane[face_index] == kind_index, incoming[face_index], jnp.zeros_like(incoming[face_index]))
            accumulated = accumulated + jnp.einsum("ji,jxy->ixy", coupling_table[kind_index, face_index].astype(jnp.float32), masked.astype(jnp.float32), precision=lax.Precision.HIGHEST)
    return accumulated


def apply_inverse(residual, kinds_plane, inverse_table):
    result = jnp.zeros(residual.shape, jnp.float32)
    for kind_index in range(KD):
        masked = jnp.where(kinds_plane[None] == kind_index, residual, jnp.zeros_like(residual))
        result = result + jnp.einsum("ij,jxy->ixy", inverse_table[kind_index].astype(jnp.float32), masked.astype(jnp.float32), precision=lax.Precision.HIGHEST)
    return result


def half_sweep(iterate, right_side, inverse_table, coupling_table, block_kind, face_kind, forward):
    sweep_low, sweep_high, low_x, high_x, low_y, high_y = face_traces(iterate)
    from_xlow = from_below(high_x, 2)
    from_xhigh = from_above(low_x, 2)
    from_ylow = from_below(high_y, 3)
    from_yhigh = from_above(low_y, 3)
    if forward:
        other_side = from_above(sweep_low, 0)
    else:
        other_side = from_below(sweep_high, 0)
    width_x = iterate.shape[2]
    width_y = iterate.shape[3]

    def advance(front_trace, inputs):
        rhs_plane, kinds_plane, faces_plane, other_plane, xlow_plane, xhigh_plane, ylow_plane, yhigh_plane = inputs
        if forward:
            incoming = [front_trace, other_plane, xlow_plane, xhigh_plane, ylow_plane, yhigh_plane]
        else:
            incoming = [other_plane, front_trace, xlow_plane, xhigh_plane, ylow_plane, yhigh_plane]
        residual = (rhs_plane - couple_terms(incoming, faces_plane, coupling_table)).astype(jnp.bfloat16)
        updated = apply_inverse(residual, kinds_plane, inverse_table)
        node_view = updated.reshape(NVAR, NP, NP * NP, width_x, width_y)
        picked = node_view[:, NP - 1] if forward else node_view[:, 0]
        return picked.reshape(TRACE, width_x, width_y).astype(jnp.bfloat16), updated

    start_trace = jnp.zeros((TRACE, width_x, width_y), jnp.bfloat16)
    _, plane_stack = lax.scan(advance, start_trace, (right_side, block_kind, face_kind, other_side, from_xlow, from_xhigh, from_ylow, from_yhigh), reverse=not forward)
    return plane_stack


def reference(right_side, inverse_table, coupling_table, block_kind, face_kind):
    iterate = jnp.zeros(right_side.shape, jnp.float32)
    for sweep_index in range(SWEEPS):
        iterate = half_sweep(iterate, right_side, inverse_table, coupling_table, block_kind, face_kind, True)
        iterate = half_sweep(iterate, right_side, inverse_table, coupling_table, block_kind, face_kind, False)
    return iterate
```

```python
import functools
import jax
import jax.numpy as jnp
from jax import lax
from jax.experimental import pallas as pl
from jax.experimental.pallas import tpu as pltpu
from jax.sharding import PartitionSpec as P

NVAR = 5
NP = 4
BLOCK = 320
TRACE = 80
KD = 4
KC = 2
SWEEPS = 2
HALVES = 2 * SWEEPS
LANES = 128
GROUP = 4
MESH = pl.DeviceIdType.MESH
F32 = jnp.float32
BF16 = jnp.bfloat16


def kernel(
    rows,
    rhs_ref,
    inv_ref,
    lat_ref,
    chain_ref,
    kind_ref,
    face_ref,
    out_ref,
    u_ref,
    base_ref,
    prod_ref,
    tr_ref,
    lat_stack,
    chain_stack,
    inv_stack,
    front_in,
    front_out,
    x_in,
    x_out,
    y_in,
    y_out,
    front_send,
    front_recv,
    x_send,
    x_recv,
    y_send,
    y_recv,
):
    groups = rows // GROUP
    places = {}
    for name in ("sweep", "cx", "cy"):
        places[name] = (lax.axis_index(name), lax.axis_size(name))

    def has(name, step):
        spot, count = places[name]
        return spot < count - 1 if step > 0 else spot > 0

    def partner(name, step):
        return {name: places[name][0] + step}

    front_in[...] = jnp.zeros(front_in.shape, BF16)
    x_in[...] = jnp.zeros(x_in.shape, BF16)
    y_in[...] = jnp.zeros(y_in.shape, BF16)
    barrier = pltpu.get_barrier_semaphore()
    total = 0
    for name in ("sweep", "cx", "cy"):
        for step in (-1, 1):
            exists = has(name, step)
            total = total + jnp.where(exists, 1, 0)

            @pl.when(exists)
            def _():
                pl.semaphore_signal(
                    barrier, inc=1, device_id=partner(name, step), device_id_type=MESH
                )

    pl.semaphore_wait(barrier, total)

    lane = lax.broadcasted_iota(jnp.int32, (TRACE, LANES), 1)

    def front_copy(half, group, step):
        return pltpu.make_async_remote_copy(
            src_ref=front_out.at[half, group],
            dst_ref=front_in.at[half, group],
            send_sem=front_send.at[half, group],
            recv_sem=front_recv.at[half, group],
            device_id=partner("sweep", step),
            device_id_type=MESH,
        )

    def x_copy(half, side):
        return pltpu.make_async_remote_copy(
            src_ref=x_out.at[half, side],
            dst_ref=x_in.at[half, 1 - side],
            send_sem=x_send.at[half, side],
            recv_sem=x_recv.at[half, 1 - side],
            device_id=partner("cx", 2 * side - 1),
            device_id_type=MESH,
        )

    def y_copy(half, side):
        return pltpu.make_async_remote_copy(
            src_ref=y_out.at[half, side],
            dst_ref=y_in.at[half, 1 - side],
            send_sem=y_send.at[half, side],
            recv_sem=y_recv.at[half, 1 - side],
            device_id=partner("cy", 2 * side - 1),
            device_id_type=MESH,
        )

    def rhs_row(row):
        return rhs_ref[pl.ds(row, BLOCK, stride=rows), :]

    def put_masked(stack, place, lanes, value, face, row):
        one = face_ref[face, row : row + 1, :].astype(F32)
        stack[pl.ds(place, TRACE), lanes] = value * (1.0 - one).astype(BF16)
        stack[pl.ds(place + TRACE, TRACE), lanes] = value * one.astype(BF16)

    def edge_x(row, side):
        first = (NP - 1) * NP * side
        for node in range(NP):
            tr_ref[pl.ds(node, NVAR * NP, stride=NP), :] = u_ref[
                row, pl.ds(first + node, NVAR * NP, stride=NP * NP), :
            ]
        return tr_ref[...]

    def edge_y(row, side):
        return u_ref[row, pl.ds((NP - 1) * side, TRACE, stride=NP), :]

    def lateral(half, group):
        for local in range(GROUP):
            row = group * GROUP + local
            lanes = slice(local * LANES, (local + 1) * LANES)
            if row > 0:
                from_xlow = edge_x(row - 1, 1).astype(BF16)
            else:
                from_xlow = x_in[half, 0]
            put_masked(lat_stack, 0, lanes, from_xlow, 2, row)
            if row < rows - 1:
                from_xhigh = edge_x(row + 1, 0).astype(BF16)
            else:
                from_xhigh = x_in[half, 1]
            put_masked(lat_stack, 2 * TRACE, lanes, from_xhigh, 3, row)
            seen = pltpu.roll(y_in[half, 0].astype(F32), (LANES - row) % LANES, 1)
            own = pltpu.roll(edge_y(row, 1), 1, 1)
            put_masked(
                lat_stack, 4 * TRACE, lanes, jnp.where(lane == 0, seen, own).astype(BF16), 4, row
            )
            seen = pltpu.roll(y_in[half, 1].astype(F32), LANES - 1 - row, 1)
            own = pltpu.roll(edge_y(row, 0), LANES - 1, 1)
            put_masked(
                lat_stack,
                6 * TRACE,
                lanes,
                jnp.where(lane == LANES - 1, seen, own).astype(BF16),
                5,
                row,
            )
        product = jnp.dot(lat_ref[...], lat_stack[...], preferred_element_type=F32)
        for local in range(GROUP):
            row = group * GROUP + local
            base_ref[row] = (
                rhs_row(row)
                - product[:, local * LANES : (local + 1) * LANES]
                - prod_ref[row]
            )

    for half in range(HALVES):
        forward = half % 2 == 0
        step = 1 if forward else -1
        upstream = has("sweep", -step)
        downstream = has("sweep", step)
        if half > 0:
            for side in range(2):

                @pl.when(has("cx", 2 * side - 1))
                def _():
                    x_copy(half - 1, 1 - side).wait_recv()

                @pl.when(has("cy", 2 * side - 1))
                def _():
                    y_copy(half - 1, 1 - side).wait_recv()

            for group in range(groups):
                lateral(half - 1, group)
        for group in range(groups):

            @pl.when(upstream)
            def _():
                front_copy(half, group, step).wait_recv()

            for local in range(GROUP):
                row = group * GROUP + local
                lanes = slice(local * LANES, (local + 1) * LANES)
                put_masked(
                    chain_stack, 0, lanes, front_in[half, group, local], 0 if forward else 1, row
                )
            product = jnp.dot(
                chain_ref[0 if forward else 1], chain_stack[...], preferred_element_type=F32
            )
            for local in range(GROUP):
                row = group * GROUP + local
                lanes = slice(local * LANES, (local + 1) * LANES)
                part = product[:, lanes]
                prod_ref[row] = part
                before = rhs_row(row) if half == 0 else base_ref[row]
                residual = (before - part).astype(BF16)
                kinds = kind_ref[row : row + 1, :]
                for kind in range(KD):
                    mask = jnp.where(kinds == kind, 1.0, 0.0).astype(BF16)
                    inv_stack[kind * BLOCK : (kind + 1) * BLOCK, lanes] = residual * mask
            updated = jnp.dot(inv_ref[...], inv_stack[...], preferred_element_type=F32)
            for local in range(GROUP):
                row = group * GROUP + local
                value = updated[:, local * LANES : (local + 1) * LANES]
                if half == HALVES - 1:
                    out_ref[pl.ds(row, BLOCK, stride=rows), :] = value
                else:
                    u_ref[row] = value
                first = NP * NP * (NP - 1) if forward else 0
                for var in range(NVAR):
                    start = var * NP * NP * NP + first
                    front_out[half, group, local, var * NP * NP : (var + 1) * NP * NP, :] = value[
                        start : start + NP * NP, :
                    ].astype(BF16)

            @pl.when(downstream)
            def _():
                front_copy(half, group, step).start()

        if half < HALVES - 1:
            for side in range(2):
                packed = jnp.zeros((TRACE, LANES), F32)
                for row in range(rows):
                    turned = pltpu.roll(edge_y(row, side), (row + side) % LANES, 1)
                    packed = jnp.where(lane == row, turned, packed)
                y_out[half, side] = packed.astype(BF16)

                @pl.when(has("cy", 2 * side - 1))
                def _():
                    y_copy(half, side).start()

                x_out[half, side] = edge_x((rows - 1) * side, side).astype(BF16)

                @pl.when(has("cx", 2 * side - 1))
                def _():
                    x_copy(half, side).start()

    for half in range(HALVES):
        step = 1 if half % 2 == 0 else -1

        @pl.when(has("sweep", step))
        def _():
            for group in range(groups):
                front_copy(half, group, step).wait_send()

        if half < HALVES - 1:
            for side in range(2):

                @pl.when(has("cy", 2 * side - 1))
                def _():
                    y_copy(half, side).wait_send()

                @pl.when(has("cx", 2 * side - 1))
                def _():
                    x_copy(half, side).wait_send()


def shards(right_side, inverse_table, coupling_table, block_kind, face_kind):
    _, _, rows, width_y = right_side.shape
    groups = rows // GROUP
    columns = GROUP * LANES
    inverse_wide = jnp.transpose(inverse_table, (1, 0, 2)).reshape(BLOCK, KD * BLOCK)
    coupling_wide = jnp.transpose(coupling_table, (3, 1, 0, 2))
    chain_wide = jnp.transpose(coupling_table[:, :2], (1, 3, 0, 2)).reshape(2, BLOCK, KC * TRACE)
    lateral_wide = coupling_wide[:, 2:].reshape(BLOCK, 4 * KC * TRACE)
    vmem = pl.BlockSpec(memory_space=pltpu.VMEM)
    result = pl.pallas_call(
        functools.partial(kernel, rows),
        out_shape=jax.ShapeDtypeStruct((BLOCK * rows, LANES), F32),
        in_specs=[vmem] * 6,
        out_specs=vmem,
        scratch_shapes=[
            pltpu.VMEM((rows, BLOCK, LANES), F32),
            pltpu.VMEM((rows, BLOCK, LANES), F32),
            pltpu.VMEM((rows, BLOCK, LANES), F32),
            pltpu.VMEM((TRACE, LANES), F32),
            pltpu.VMEM((4 * KC * TRACE, columns), BF16),
            pltpu.VMEM((KC * TRACE, columns), BF16),
            pltpu.VMEM((KD * BLOCK, columns), BF16),
            pltpu.VMEM((HALVES, groups, GROUP, TRACE, LANES), BF16),
            pltpu.VMEM((HALVES, groups, GROUP, TRACE, LANES), BF16),
            pltpu.VMEM((HALVES - 1, 2, TRACE, LANES), BF16),
            pltpu.VMEM((HALVES - 1, 2, TRACE, LANES), BF16),
            pltpu.VMEM((HALVES - 1, 2, TRACE, LANES), BF16),
            pltpu.VMEM((HALVES - 1, 2, TRACE, LANES), BF16),
            pltpu.SemaphoreType.DMA((HALVES, groups)),
            pltpu.SemaphoreType.DMA((HALVES, groups)),
            pltpu.SemaphoreType.DMA((HALVES - 1, 2)),
            pltpu.SemaphoreType.DMA((HALVES - 1, 2)),
            pltpu.SemaphoreType.DMA((HALVES - 1, 2)),
            pltpu.SemaphoreType.DMA((HALVES - 1, 2)),
        ],
        compiler_params=pltpu.CompilerParams(
            collective_id=0, has_side_effects=True, vmem_limit_bytes=48 << 20
        ),
    )(
        right_side.reshape(BLOCK * rows, width_y),
        inverse_wide,
        lateral_wide,
        chain_wide,
        block_kind.reshape(rows, width_y),
        face_kind.reshape(6, rows, width_y),
    )
    return result.reshape(right_side.shape)


def solution(mesh):
    in_specs = (
        P("sweep", None, "cx", "cy"),
        P(),
        P(),
        P("sweep", "cx", "cy"),
        P("sweep", None, "cx", "cy"),
    )
    out_specs = P("sweep", None, "cx", "cy")
    return jax.shard_map(shards, mesh=mesh, in_specs=in_specs, out_specs=out_specs, check_vma=False)
```

```python
import functools
import jax
import jax.numpy as jnp
from jax import lax
from jax.experimental import pallas as pl
from jax.experimental.pallas import tpu as pltpu
from jax.sharding import PartitionSpec as P

NVAR = 5
NP = 4
BLOCK = 320
TRACE = 80
KD = 4
KC = 2
SWEEPS = 2
HALVES = 2 * SWEEPS
LANES = 128
WIDE = 256
GROUP = 4
MESH = pl.DeviceIdType.MESH
F32 = jnp.float32
BF16 = jnp.bfloat16


def kernel(
    rows,
    rhs_ref,
    table_ref,
    coupling_ref,
    kind_ref,
    face_ref,
    out_ref,
    inv_ref,
    tall_ref,
    lat_ref,
    chain_ref,
    u_ref,
    base_ref,
    prod_ref,
    tr_ref,
    lat_stack,
    chain_stack,
    inv_stack,
    front_in,
    front_out,
    x_in,
    x_out,
    y_in,
    y_out,
    front_send,
    front_recv,
    x_send,
    x_recv,
    y_send,
    y_recv,
):
    groups = rows // GROUP
    places = {}
    for name in ("sweep", "cx", "cy"):
        places[name] = (lax.axis_index(name), lax.axis_size(name))

    def has(name, step):
        spot, count = places[name]
        return spot < count - 1 if step > 0 else spot > 0

    def partner(name, step):
        return {name: places[name][0] + step}

    front_in[...] = jnp.zeros(front_in.shape, BF16)
    x_in[...] = jnp.zeros(x_in.shape, BF16)
    y_in[...] = jnp.zeros(y_in.shape, BF16)
    barrier = pltpu.get_barrier_semaphore()
    total = 0
    for name in ("sweep", "cx", "cy"):
        for step in (-1, 1):
            exists = has(name, step)
            total = total + jnp.where(exists, 1, 0)

            @pl.when(exists)
            def _():
                pl.semaphore_signal(
                    barrier, inc=1, device_id=partner(name, step), device_id_type=MESH
                )

    for kind in range(KD):
        inv_ref[:, kind * WIDE : (kind + 1) * WIDE] = table_ref[kind, :, :WIDE]
    for pair in range(KD // 2):
        inv_ref[:, KD * WIDE + pair * LANES : KD * WIDE + (pair + 1) * LANES] = jnp.concatenate(
            [table_ref[2 * pair, :, WIDE:], table_ref[2 * pair + 1, :, WIDE:]], axis=1
        )
    for kind in range(KC):
        tall_ref[kind * 4 * TRACE : (kind + 1) * 4 * TRACE, :BLOCK] = coupling_ref[
            (kind * 6 + 2) * TRACE : (kind * 6 + 6) * TRACE, :
        ]
    lat_ref[...] = jnp.transpose(tall_ref[...])[:BLOCK]
    for face in range(2):
        for kind in range(KC):
            tall_ref[kind * TRACE : (kind + 1) * TRACE, :BLOCK] = coupling_ref[
                (kind * 6 + face) * TRACE : (kind * 6 + face + 1) * TRACE, :
            ]
        chain_ref[face] = jnp.transpose(tall_ref[: 2 * LANES, :])[:BLOCK, : KC * TRACE]

    pl.semaphore_wait(barrier, total)

    lane = lax.broadcasted_iota(jnp.int32, (TRACE, LANES), 1)

    def front_copy(half, group, step):
        return pltpu.make_async_remote_copy(
            src_ref=front_out.at[half, group],
            dst_ref=front_in.at[half, group],
            send_sem=front_send.at[half, group],
            recv_sem=front_recv.at[half, group],
            device_id=partner("sweep", step),
            device_id_type=MESH,
        )

    def x_copy(half, side):
        return pltpu.make_async_remote_copy(
            src_ref=x_out.at[half, side],
            dst_ref=x_in.at[half, 1 - side],
            send_sem=x_send.at[half, side],
            recv_sem=x_recv.at[half, 1 - side],
            device_id=partner("cx", 2 * side - 1),
            device_id_type=MESH,
        )

    def y_copy(half, side):
        return pltpu.make_async_remote_copy(
            src_ref=y_out.at[half, side],
            dst_ref=y_in.at[half, 1 - side],
            send_sem=y_send.at[half, side],
            recv_sem=y_recv.at[half, 1 - side],
            device_id=partner("cy", 2 * side - 1),
            device_id_type=MESH,
        )

    def rhs_row(row):
        return rhs_ref[pl.ds(row, BLOCK, stride=rows), :]

    def put_masked(stack, place, lanes, value, face, row, apart=TRACE):
        one = face_ref[face, row : row + 1, :].astype(F32)
        stack[pl.ds(place, TRACE), lanes] = value * (1.0 - one).astype(BF16)
        stack[pl.ds(place + apart, TRACE), lanes] = value * one.astype(BF16)

    def edge_x(row, side):
        first = (NP - 1) * NP * side
        for node in range(NP):
            tr_ref[pl.ds(node, NVAR * NP, stride=NP), :] = u_ref[
                row, pl.ds(first + node, NVAR * NP, stride=NP * NP), :
            ]
        return tr_ref[...]

    def edge_y(row, side):
        return u_ref[row, pl.ds((NP - 1) * side, TRACE, stride=NP), :]

    def lateral(half, group):
        for local in range(GROUP):
            row = group * GROUP + local
            lanes = slice(local * LANES, (local + 1) * LANES)
            if row > 0:
                from_xlow = edge_x(row - 1, 1).astype(BF16)
            else:
                from_xlow = x_in[half, 0]
            put_masked(lat_stack, 0, lanes, from_xlow, 2, row, 4 * TRACE)
            if row < rows - 1:
                from_xhigh = edge_x(row + 1, 0).astype(BF16)
            else:
                from_xhigh = x_in[half, 1]
            put_masked(lat_stack, TRACE, lanes, from_xhigh, 3, row, 4 * TRACE)
            seen = pltpu.roll(y_in[half, 0].astype(F32), (LANES - row) % LANES, 1)
            own = pltpu.roll(edge_y(row, 1), 1, 1)
            from_ylow = jnp.where(lane == 0, seen, own).astype(BF16)
            put_masked(lat_stack, 2 * TRACE, lanes, from_ylow, 4, row, 4 * TRACE)
            seen = pltpu.roll(y_in[half, 1].astype(F32), LANES - 1 - row, 1)
            own = pltpu.roll(edge_y(row, 0), LANES - 1, 1)
            from_yhigh = jnp.where(lane == LANES - 1, seen, own).astype(BF16)
            put_masked(lat_stack, 3 * TRACE, lanes, from_yhigh, 5, row, 4 * TRACE)
        product = jnp.dot(lat_ref[...], lat_stack[...], preferred_element_type=F32)
        for local in range(GROUP):
            row = group * GROUP + local
            base_ref[row] = (
                rhs_row(row)
                - product[:, local * LANES : (local + 1) * LANES]
                - prod_ref[row]
            )

    for half in range(HALVES):
        forward = half % 2 == 0
        step = 1 if forward else -1
        upstream = has("sweep", -step)
        downstream = has("sweep", step)
        if half > 0:
            for side in range(2):

                @pl.when(has("cx", 2 * side - 1))
                def _():
                    x_copy(half - 1, 1 - side).wait_recv()

                @pl.when(has("cy", 2 * side - 1))
                def _():
                    y_copy(half - 1, 1 - side).wait_recv()

            for group in range(groups):
                lateral(half - 1, group)
        for group in range(groups):

            @pl.when(upstream)
            def _():
                front_copy(half, group, step).wait_recv()

            for local in range(GROUP):
                row = group * GROUP + local
                lanes = slice(local * LANES, (local + 1) * LANES)
                put_masked(
                    chain_stack, 0, lanes, front_in[half, group, local], 0 if forward else 1, row
                )
            product = jnp.dot(
                chain_ref[0 if forward else 1], chain_stack[...], preferred_element_type=F32
            )
            for local in range(GROUP):
                row = group * GROUP + local
                lanes = slice(local * LANES, (local + 1) * LANES)
                part = product[:, lanes]
                prod_ref[row] = part
                before = rhs_row(row) if half == 0 else base_ref[row]
                residual = (before - part).astype(BF16)
                kinds = kind_ref[row : row + 1, :]
                for kind in range(KD):
                    mask = jnp.where(kinds == kind, 1.0, 0.0).astype(BF16)
                    masked = residual * mask
                    rest = KD * WIDE + kind * (BLOCK - WIDE)
                    inv_stack[kind * WIDE : (kind + 1) * WIDE, lanes] = masked[:WIDE]
                    inv_stack[rest : rest + BLOCK - WIDE, lanes] = masked[WIDE:]
            updated = jnp.dot(inv_ref[...], inv_stack[...], preferred_element_type=F32)
            for local in range(GROUP):
                row = group * GROUP + local
                value = updated[:, local * LANES : (local + 1) * LANES]
                if half == HALVES - 1:
                    out_ref[pl.ds(row, BLOCK, stride=rows), :] = value
                else:
                    u_ref[row] = value
                first = NP * NP * (NP - 1) if forward else 0
                for var in range(NVAR):
                    start = var * NP * NP * NP + first
                    front_out[half, group, local, var * NP * NP : (var + 1) * NP * NP, :] = value[
                        start : start + NP * NP, :
                    ].astype(BF16)

            @pl.when(downstream)
            def _():
                front_copy(half, group, step).start()

        if half < HALVES - 1:
            for side in range(2):
                packed = jnp.zeros((TRACE, LANES), F32)
                for row in range(rows):
                    turned = pltpu.roll(edge_y(row, side), (row + side) % LANES, 1)
                    packed = jnp.where(lane == row, turned, packed)
                y_out[half, side] = packed.astype(BF16)

                @pl.when(has("cy", 2 * side - 1))
                def _():
                    y_copy(half, side).start()

                x_out[half, side] = edge_x((rows - 1) * side, side).astype(BF16)

                @pl.when(has("cx", 2 * side - 1))
                def _():
                    x_copy(half, side).start()

    for half in range(HALVES):
        step = 1 if half % 2 == 0 else -1

        @pl.when(has("sweep", step))
        def _():
            for group in range(groups):
                front_copy(half, group, step).wait_send()

        if half < HALVES - 1:
            for side in range(2):

                @pl.when(has("cy", 2 * side - 1))
                def _():
                    y_copy(half, side).wait_send()

                @pl.when(has("cx", 2 * side - 1))
                def _():
                    x_copy(half, side).wait_send()


def shards(right_side, inverse_table, coupling_table, block_kind, face_kind):
    _, _, rows, width_y = right_side.shape
    groups = rows // GROUP
    columns = GROUP * LANES
    vmem = pl.BlockSpec(memory_space=pltpu.VMEM)
    result = pl.pallas_call(
        functools.partial(kernel, rows),
        out_shape=jax.ShapeDtypeStruct((BLOCK * rows, LANES), F32),
        in_specs=[vmem] * 5,
        out_specs=vmem,
        scratch_shapes=[
            pltpu.VMEM((BLOCK, KD * BLOCK), BF16),
            pltpu.VMEM((4 * KC * TRACE, 3 * LANES), BF16),
            pltpu.VMEM((BLOCK, 4 * KC * TRACE), BF16),
            pltpu.VMEM((2, BLOCK, KC * TRACE), BF16),
            pltpu.VMEM((rows, BLOCK, LANES), F32),
            pltpu.VMEM((rows, BLOCK, LANES), F32),
            pltpu.VMEM((rows, BLOCK, LANES), F32),
            pltpu.VMEM((TRACE, LANES), F32),
            pltpu.VMEM((4 * KC * TRACE, columns), BF16),
            pltpu.VMEM((KC * TRACE, columns), BF16),
            pltpu.VMEM((KD * BLOCK, columns), BF16),
            pltpu.VMEM((HALVES, groups, GROUP, TRACE, LANES), BF16),
            pltpu.VMEM((HALVES, groups, GROUP, TRACE, LANES), BF16),
            pltpu.VMEM((HALVES - 1, 2, TRACE, LANES), BF16),
            pltpu.VMEM((HALVES - 1, 2, TRACE, LANES), BF16),
            pltpu.VMEM((HALVES - 1, 2, TRACE, LANES), BF16),
            pltpu.VMEM((HALVES - 1, 2, TRACE, LANES), BF16),
            pltpu.SemaphoreType.DMA((HALVES, groups)),
            pltpu.SemaphoreType.DMA((HALVES, groups)),
            pltpu.SemaphoreType.DMA((HALVES - 1, 2)),
            pltpu.SemaphoreType.DMA((HALVES - 1, 2)),
            pltpu.SemaphoreType.DMA((HALVES - 1, 2)),
            pltpu.SemaphoreType.DMA((HALVES - 1, 2)),
        ],
        compiler_params=pltpu.CompilerParams(
            collective_id=0, has_side_effects=True, vmem_limit_bytes=48 << 20
        ),
    )(
        right_side.reshape(BLOCK * rows, width_y),
        inverse_table,
        coupling_table.reshape(KC * 6 * TRACE, BLOCK),
        block_kind.reshape(rows, width_y),
        face_kind.reshape(6, rows, width_y),
    )
    return result.reshape(right_side.shape)


def solution(mesh):
    in_specs = (
        P("sweep", None, "cx", "cy"),
        P(),
        P(),
        P("sweep", "cx", "cy"),
        P("sweep", None, "cx", "cy"),
    )
    out_specs = P("sweep", None, "cx", "cy")
    return jax.shard_map(shards, mesh=mesh, in_specs=in_specs, out_specs=out_specs, check_vma=False)
```

```python
import functools
import jax
import jax.numpy as jnp
from jax import lax
from jax.experimental import pallas as pl
from jax.experimental.pallas import tpu as pltpu
from jax.sharding import PartitionSpec as P

NVAR = 5
NP = 4
BLOCK = 320
TRACE = 80
KD = 4
KC = 2
SWEEPS = 2
HALVES = 2 * SWEEPS
LANES = 128
WIDE = 256
GROUP = 2
MESH = pl.DeviceIdType.MESH
F32 = jnp.float32
BF16 = jnp.bfloat16


def kernel(
    rows,
    rhs_ref,
    table_ref,
    coupling_ref,
    kind_ref,
    face_ref,
    out_ref,
    inv_ref,
    tall_ref,
    lat_ref,
    chain_ref,
    u_ref,
    base_ref,
    prod_ref,
    tr_ref,
    lat_stack,
    chain_stack,
    inv_stack,
    front_in,
    front_out,
    x_low,
    x_high,
    y_in,
    y_out,
    front_send,
    front_recv,
    x_send,
    x_recv,
    y_send,
    y_recv,
):
    groups = rows // GROUP
    places = {}
    for name in ("sweep", "cx", "cy"):
        places[name] = (lax.axis_index(name), lax.axis_size(name))

    def has(name, step):
        spot, count = places[name]
        return spot < count - 1 if step > 0 else spot > 0

    def partner(name, step):
        return {name: places[name][0] + step}

    for half in range(HALVES - 1):
        x_high[half, 0] = jnp.zeros((TRACE, LANES), BF16)
        x_low[half, rows + 1] = jnp.zeros((TRACE, LANES), BF16)
    for side in range(2):

        @pl.when(jnp.logical_not(has("cy", 2 * side - 1)))
        def _():
            for half in range(HALVES - 1):
                y_in[half, side] = jnp.zeros((groups, TRACE, LANES), BF16)

    barrier = pltpu.get_barrier_semaphore()
    total = 0
    for name in ("sweep", "cx", "cy"):
        for step in (-1, 1):
            exists = has(name, step)
            total = total + jnp.where(exists, 1, 0)

            @pl.when(exists)
            def _():
                pl.semaphore_signal(
                    barrier, inc=1, device_id=partner(name, step), device_id_type=MESH
                )

    for kind in range(KD):
        inv_ref[:, kind * WIDE : (kind + 1) * WIDE] = table_ref[kind, :, :WIDE]
    for pair in range(KD // 2):
        inv_ref[:, KD * WIDE + pair * LANES : KD * WIDE + (pair + 1) * LANES] = jnp.concatenate(
            [table_ref[2 * pair, :, WIDE:], table_ref[2 * pair + 1, :, WIDE:]], axis=1
        )
    pl.semaphore_wait(barrier, total)

    def lay_out_coupling():
        for kind in range(KC):
            tall_ref[kind * 4 * TRACE : (kind + 1) * 4 * TRACE, :BLOCK] = coupling_ref[
                (kind * 6 + 2) * TRACE : (kind * 6 + 6) * TRACE, :
            ]
        lat_ref[...] = jnp.transpose(tall_ref[...])[:BLOCK]
        for face in range(2):
            for kind in range(KC):
                tall_ref[kind * TRACE : (kind + 1) * TRACE, :BLOCK] = coupling_ref[
                    (kind * 6 + face) * TRACE : (kind * 6 + face + 1) * TRACE, :
                ]
            chain_ref[face] = jnp.transpose(tall_ref[: 2 * LANES, :])[:BLOCK, : KC * TRACE]

    lane = lax.broadcasted_iota(jnp.int32, (TRACE, LANES), 1)
    flip = lax.rem(places["cx"][0], 2)

    def place_of(turn):
        return turn + flip * (groups - 1 - 2 * turn)

    def front_copy(half, group, step):
        return pltpu.make_async_remote_copy(
            src_ref=front_out.at[half, group],
            dst_ref=front_in.at[half, group],
            send_sem=front_send.at[half, group],
            recv_sem=front_recv.at[half, group],
            device_id=partner("sweep", step),
            device_id_type=MESH,
        )

    def x_copy(half, side):
        source, target = (x_low.at[half, 1], x_low.at[half, rows + 1])
        if side == 1:
            source, target = (x_high.at[half, rows], x_high.at[half, 0])
        return pltpu.make_async_remote_copy(
            src_ref=source,
            dst_ref=target,
            send_sem=x_send.at[half, side],
            recv_sem=x_recv.at[half, 1 - side],
            device_id=partner("cx", 2 * side - 1),
            device_id_type=MESH,
        )

    def y_copy(half, side, group):
        return pltpu.make_async_remote_copy(
            src_ref=y_out.at[half, side, group],
            dst_ref=y_in.at[half, 1 - side, group],
            send_sem=y_send.at[half, side, group],
            recv_sem=y_recv.at[half, 1 - side, group],
            device_id=partner("cy", 2 * side - 1),
            device_id_type=MESH,
        )

    def x_here(side, group):
        return jnp.logical_and(has("cx", 2 * side - 1), group == (groups - 1) * side)

    def rhs_row(row):
        return rhs_ref[pl.ds(row, BLOCK, stride=rows), :]

    def put_masked(stack, place, lanes, value, face, row, apart):
        one = face_ref[face, pl.ds(row, 1), :].astype(F32)
        stack[place : place + TRACE, lanes] = value * (1.0 - one).astype(BF16)
        stack[place + apart : place + apart + TRACE, lanes] = value * one.astype(BF16)

    def edge_x(row, local, side):
        first = (NP - 1) * NP * side
        for node in range(NP):
            tr_ref[local, side, pl.ds(node, NVAR * NP, stride=NP), :] = u_ref[
                row, pl.ds(first + node, NVAR * NP, stride=NP * NP), :
            ]
        return tr_ref[local, side].astype(BF16)

    def edge_y(row, side):
        return u_ref[row, pl.ds((NP - 1) * side, TRACE, stride=NP), :]

    def turned(value, shift):
        return pltpu.roll(value, shift % LANES, 1) if shift % LANES else value

    def lateral(half, group):
        for side in range(2):

            @pl.when(x_here(side, group))
            def _():
                x_copy(half, 1 - side).wait_recv()

            @pl.when(has("cy", 2 * side - 1))
            def _():
                y_copy(half, 1 - side, group).wait_recv()

        for local in range(GROUP):
            row = group * GROUP + local
            lanes = slice(local * LANES, (local + 1) * LANES)
            apart = 4 * TRACE
            put_masked(lat_stack, 0, lanes, x_high[half, row], 2, row, apart)
            put_masked(lat_stack, TRACE, lanes, x_low[half, row + 2], 3, row, apart)
            seen = turned(y_in[half, 0, group].astype(F32), -local)
            from_ylow = jnp.where(lane == 0, seen, turned(edge_y(row, 1), 1))
            put_masked(lat_stack, 2 * TRACE, lanes, from_ylow.astype(BF16), 4, row, apart)
            seen = turned(y_in[half, 1, group].astype(F32), -1 - local)
            from_yhigh = jnp.where(lane == LANES - 1, seen, turned(edge_y(row, 0), -1))
            put_masked(lat_stack, 3 * TRACE, lanes, from_yhigh.astype(BF16), 5, row, apart)
        product = jnp.dot(lat_ref[...], lat_stack[...], preferred_element_type=F32)
        for local in range(GROUP):
            row = group * GROUP + local
            lanes = slice(local * LANES, (local + 1) * LANES)
            base_ref[row] = rhs_row(row) - product[:, lanes] - prod_ref[row]

    def update(half, group, upstream, downstream):
        forward = half % 2 == 0
        step = 1 if forward else -1

        @pl.when(upstream)
        def _():
            front_copy(half, group, step).wait_recv()
            face = 0 if forward else 1
            for local in range(GROUP):
                row = group * GROUP + local
                lanes = slice(local * LANES, (local + 1) * LANES)
                put_masked(
                    chain_stack, 0, lanes, front_in[half, group, local], face, row, TRACE
                )
            product = jnp.dot(chain_ref[face], chain_stack[...], preferred_element_type=F32)
            for local in range(GROUP):
                row = group * GROUP + local
                part = product[:, local * LANES : (local + 1) * LANES]
                prod_ref[row] = part
                base_ref[row] = (rhs_row(row) if half == 0 else base_ref[row]) - part

        @pl.when(jnp.logical_not(upstream))
        def _():
            for local in range(GROUP):
                row = group * GROUP + local
                prod_ref[row] = jnp.zeros((BLOCK, LANES), F32)
                if half == 0:
                    base_ref[row] = rhs_row(row)

        for local in range(GROUP):
            row = group * GROUP + local
            lanes = slice(local * LANES, (local + 1) * LANES)
            residual = base_ref[row].astype(BF16)
            kinds = kind_ref[pl.ds(row, 1), :]
            for kind in range(KD):
                masked = residual * jnp.where(kinds == kind, 1.0, 0.0).astype(BF16)
                rest = KD * WIDE + kind * (BLOCK - WIDE)
                inv_stack[kind * WIDE : (kind + 1) * WIDE, lanes] = masked[:WIDE]
                inv_stack[rest : rest + BLOCK - WIDE, lanes] = masked[WIDE:]
        updated = jnp.dot(inv_ref[...], inv_stack[...], preferred_element_type=F32)
        first = NP * NP * (NP - 1) if forward else 0
        for local in range(GROUP):
            value = updated[:, local * LANES : (local + 1) * LANES]
            for var in range(NVAR):
                start = var * NP * NP * NP + first
                front_out[half, group, local, var * NP * NP : (var + 1) * NP * NP, :] = value[
                    start : start + NP * NP, :
                ].astype(BF16)

        @pl.when(downstream)
        def _():
            front_copy(half, group, step).start()

        for local in range(GROUP):
            row = group * GROUP + local
            value = updated[:, local * LANES : (local + 1) * LANES]
            if half == HALVES - 1:
                out_ref[pl.ds(row, BLOCK, stride=rows), :] = value
            else:
                u_ref[row] = value
        if half == HALVES - 1:
            return
        for side in range(2):
            first_row = edge_y(group * GROUP, side)
            packed = turned(first_row, side)
            for local in range(1, GROUP):
                other = turned(edge_y(group * GROUP + local, side), local + side)
                packed = jnp.where(lane == local, other, packed)
            y_out[half, side, group] = packed.astype(BF16)

            @pl.when(has("cy", 2 * side - 1))
            def _():
                y_copy(half, side, group).start()

        for local in range(GROUP):
            row = group * GROUP + local
            x_low[half, row + 1] = edge_x(row, local, 0)
            x_high[half, row + 1] = edge_x(row, local, 1)
        for side in range(2):

            @pl.when(x_here(side, group))
            def _():
                x_copy(half, side).start()

    for half in range(HALVES):
        step = 1 if half % 2 == 0 else -1
        upstream = has("sweep", -step)
        downstream = has("sweep", step)

        @pl.when(upstream)
        def _():
            if half == 0:
                lay_out_coupling()
            else:

                @pl.loop(0, groups)
                def _(turn):
                    lateral(half - 1, place_of(turn))

        @pl.loop(0, groups)
        def _(turn):
            group = place_of(turn)
            if half > 0:

                @pl.when(jnp.logical_not(upstream))
                def _():
                    lateral(half - 1, group)

            update(half, group, upstream, downstream)

        if half == 0:

            @pl.when(jnp.logical_not(upstream))
            def _():
                lay_out_coupling()

    for half in range(HALVES):
        step = 1 if half % 2 == 0 else -1

        @pl.when(has("sweep", step))
        def _():
            @pl.loop(0, groups)
            def _(group):
                front_copy(half, group, step).wait_send()

        if half < HALVES - 1:
            for side in range(2):

                @pl.when(has("cy", 2 * side - 1))
                def _():
                    @pl.loop(0, groups)
                    def _(group):
                        y_copy(half, side, group).wait_send()

                @pl.when(has("cx", 2 * side - 1))
                def _():
                    x_copy(half, side).wait_send()


def shards(right_side, inverse_table, coupling_table, block_kind, face_kind):
    _, _, rows, width_y = right_side.shape
    groups = rows // GROUP
    columns = GROUP * LANES
    vmem = pl.BlockSpec(memory_space=pltpu.VMEM)
    result = pl.pallas_call(
        functools.partial(kernel, rows),
        out_shape=jax.ShapeDtypeStruct((BLOCK * rows, LANES), F32),
        in_specs=[vmem] * 5,
        out_specs=vmem,
        scratch_shapes=[
            pltpu.VMEM((BLOCK, KD * BLOCK), BF16),
            pltpu.VMEM((4 * KC * TRACE, 3 * LANES), BF16),
            pltpu.VMEM((BLOCK, 4 * KC * TRACE), BF16),
            pltpu.VMEM((2, BLOCK, KC * TRACE), BF16),
            pltpu.VMEM((rows, BLOCK, LANES), F32),
            pltpu.VMEM((rows, BLOCK, LANES), F32),
            pltpu.VMEM((rows, BLOCK, LANES), F32),
            pltpu.VMEM((GROUP, 2, TRACE, LANES), F32),
            pltpu.VMEM((4 * KC * TRACE, columns), BF16),
            pltpu.VMEM((KC * TRACE, columns), BF16),
            pltpu.VMEM((KD * BLOCK, columns), BF16),
            pltpu.VMEM((HALVES, groups, GROUP, TRACE, LANES), BF16),
            pltpu.VMEM((HALVES, groups, GROUP, TRACE, LANES), BF16),
            pltpu.VMEM((HALVES - 1, rows + 2, TRACE, LANES), BF16),
            pltpu.VMEM((HALVES - 1, rows + 2, TRACE, LANES), BF16),
            pltpu.VMEM((HALVES - 1, 2, groups, TRACE, LANES), BF16),
            pltpu.VMEM((HALVES - 1, 2, groups, TRACE, LANES), BF16),
            pltpu.SemaphoreType.DMA((HALVES, groups)),
            pltpu.SemaphoreType.DMA((HALVES, groups)),
            pltpu.SemaphoreType.DMA((HALVES - 1, 2)),
            pltpu.SemaphoreType.DMA((HALVES - 1, 2)),
            pltpu.SemaphoreType.DMA((HALVES - 1, 2, groups)),
            pltpu.SemaphoreType.DMA((HALVES - 1, 2, groups)),
        ],
        compiler_params=pltpu.CompilerParams(
            collective_id=0, has_side_effects=True, vmem_limit_bytes=48 << 20
        ),
    )(
        right_side.reshape(BLOCK * rows, width_y),
        inverse_table,
        coupling_table.reshape(KC * 6 * TRACE, BLOCK),
        block_kind.reshape(rows, width_y),
        face_kind.reshape(6, rows, width_y),
    )
    return result.reshape(right_side.shape)


def solution(mesh):
    in_specs = (
        P("sweep", None, "cx", "cy"),
        P(),
        P(),
        P("sweep", "cx", "cy"),
        P("sweep", None, "cx", "cy"),
    )
    out_specs = P("sweep", None, "cx", "cy")
    return jax.shard_map(shards, mesh=mesh, in_specs=in_specs, out_specs=out_specs, check_vma=False)
```

```python
import functools
import jax
import jax.numpy as jnp
from jax import lax
from jax.experimental import pallas as pl
from jax.experimental.pallas import tpu as pltpu
from jax.sharding import PartitionSpec as P

NVAR = 5
NP = 4
BLOCK = 320
TRACE = 80
KD = 4
KC = 2
SWEEPS = 2
HALVES = 2 * SWEEPS
LANES = 128
WIDE = 256
GROUP = 2
MESH = pl.DeviceIdType.MESH
F32 = jnp.float32
BF16 = jnp.bfloat16


def kernel(
    rows,
    rhs_in,
    table_in,
    coupling_in,
    kind_in,
    face_in,
    out_ref,
    rhs_ref,
    table_ref,
    coupling_ref,
    kind_ref,
    face_ref,
    load_sem,
    inv_ref,
    tall_ref,
    wide_ref,
    u_ref,
    res_ref,
    tr_ref,
    stack,
    inv_stack,
    front_in,
    front_out,
    x_low,
    x_high,
    y_in,
    y_out,
    front_send,
    front_recv,
    x_send,
    x_recv,
    y_send,
    y_recv,
):
    groups = rows // GROUP
    loads = [
        pltpu.make_async_copy(source, target, load_sem.at[spot])
        for spot, (source, target) in enumerate(
            (
                (table_in, table_ref),
                (rhs_in, rhs_ref),
                (kind_in, kind_ref),
                (coupling_in, coupling_ref),
                (face_in, face_ref),
            )
        )
    ]
    for load in loads:
        load.start()
    places = {}
    for name in ("sweep", "cx", "cy"):
        places[name] = (lax.axis_index(name), lax.axis_size(name))

    def has(name, step):
        spot, count = places[name]
        return spot < count - 1 if step > 0 else spot > 0

    def partner(name, step):
        return {name: places[name][0] + step}

    for half in range(HALVES - 1):
        x_high[half, 0] = jnp.zeros((TRACE, LANES), BF16)
        x_low[half, rows + 1] = jnp.zeros((TRACE, LANES), BF16)
    for side in range(2):

        @pl.when(jnp.logical_not(has("cy", 2 * side - 1)))
        def _():
            for half in range(HALVES - 1):
                y_in[half, side] = jnp.zeros((groups, TRACE, LANES), BF16)

    barrier = pltpu.get_barrier_semaphore()
    total = 0
    for name in ("sweep", "cx", "cy"):
        for step in (-1, 1):
            exists = has(name, step)
            total = total + jnp.where(exists, 1, 0)

            @pl.when(exists)
            def _():
                pl.semaphore_signal(
                    barrier, inc=1, device_id=partner(name, step), device_id_type=MESH
                )

    stack[...] = jnp.zeros(stack.shape, BF16)
    loads[0].wait()
    for kind in range(KD):
        inv_ref[:, kind * WIDE : (kind + 1) * WIDE] = table_ref[kind, :, :WIDE]
    for pair in range(KD // 2):
        inv_ref[:, KD * WIDE + pair * LANES : KD * WIDE + (pair + 1) * LANES] = jnp.concatenate(
            [table_ref[2 * pair, :, WIDE:], table_ref[2 * pair + 1, :, WIDE:]], axis=1
        )
    for load in loads[1:]:
        load.wait()
    pl.semaphore_wait(barrier, total)

    def lay_out_coupling():
        tall_ref[: KC * 6 * TRACE, :BLOCK] = coupling_ref[...]
        wide_ref[...] = jnp.transpose(tall_ref[...])[:BLOCK, : KC * 6 * TRACE]

    lane = lax.broadcasted_iota(jnp.int32, (TRACE, LANES), 1)
    flip = lax.rem(places["cx"][0], 2)

    def place_of(turn):
        return turn + flip * (groups - 1 - 2 * turn)

    def front_copy(half, group, step):
        return pltpu.make_async_remote_copy(
            src_ref=front_out.at[half, group],
            dst_ref=front_in.at[half, group],
            send_sem=front_send.at[half, group],
            recv_sem=front_recv.at[half, group],
            device_id=partner("sweep", step),
            device_id_type=MESH,
        )

    def x_copy(half, side):
        source, target = (x_low.at[half, 1], x_low.at[half, rows + 1])
        if side == 1:
            source, target = (x_high.at[half, rows], x_high.at[half, 0])
        return pltpu.make_async_remote_copy(
            src_ref=source,
            dst_ref=target,
            send_sem=x_send.at[half, side],
            recv_sem=x_recv.at[half, 1 - side],
            device_id=partner("cx", 2 * side - 1),
            device_id_type=MESH,
        )

    def y_copy(half, side, group):
        return pltpu.make_async_remote_copy(
            src_ref=y_out.at[half, side, group],
            dst_ref=y_in.at[half, 1 - side, group],
            send_sem=y_send.at[half, side, group],
            recv_sem=y_recv.at[half, 1 - side, group],
            device_id=partner("cy", 2 * side - 1),
            device_id_type=MESH,
        )

    def x_here(side, group):
        return jnp.logical_and(has("cx", 2 * side - 1), group == (groups - 1) * side)

    def rhs_row(row):
        return rhs_ref[pl.ds(row, BLOCK, stride=rows), :]

    def put_masked(group, lanes, value, face, row):
        one = face_ref[face, pl.ds(row, 1), :].astype(F32)
        place = face * TRACE
        stack[group, place : place + TRACE, lanes] = value * (1.0 - one).astype(BF16)
        place = (6 + face) * TRACE
        stack[group, place : place + TRACE, lanes] = value * one.astype(BF16)

    def edge_x(row, local, side):
        first = (NP - 1) * NP * side
        for node in range(NP):
            tr_ref[local, side, pl.ds(node, NVAR * NP, stride=NP), :] = u_ref[
                row, pl.ds(first + node, NVAR * NP, stride=NP * NP), :
            ]
        return tr_ref[local, side].astype(BF16)

    def edge_y(row, side):
        return u_ref[row, pl.ds((NP - 1) * side, TRACE, stride=NP), :]

    def turned(value, shift):
        return pltpu.roll(value, shift % LANES, 1) if shift % LANES else value

    def lateral(half, group):
        for side in range(2):

            @pl.when(x_here(side, group))
            def _():
                x_copy(half, 1 - side).wait_recv()

            @pl.when(has("cy", 2 * side - 1))
            def _():
                y_copy(half, 1 - side, group).wait_recv()

        for local in range(GROUP):
            row = group * GROUP + local
            lanes = slice(local * LANES, (local + 1) * LANES)
            put_masked(group, lanes, x_high[half, row], 2, row)
            put_masked(group, lanes, x_low[half, row + 2], 3, row)
            seen = turned(y_in[half, 0, group].astype(F32), -local)
            from_ylow = jnp.where(lane == 0, seen, turned(edge_y(row, 1), 1))
            put_masked(group, lanes, from_ylow.astype(BF16), 4, row)
            seen = turned(y_in[half, 1, group].astype(F32), -1 - local)
            from_yhigh = jnp.where(lane == LANES - 1, seen, turned(edge_y(row, 0), -1))
            put_masked(group, lanes, from_yhigh.astype(BF16), 5, row)

    def update(half, group, upstream, downstream):
        forward = half % 2 == 0
        step = 1 if forward else -1

        def coupled():
            product = jnp.dot(wide_ref[...], stack[group], preferred_element_type=F32)
            for local in range(GROUP):
                row = group * GROUP + local
                part = product[:, local * LANES : (local + 1) * LANES]
                res_ref[local] = (rhs_row(row) - part).astype(BF16)

        @pl.when(upstream)
        def _():
            front_copy(half, group, step).wait_recv()
            face = 0 if forward else 1
            for local in range(GROUP):
                row = group * GROUP + local
                lanes = slice(local * LANES, (local + 1) * LANES)
                put_masked(group, lanes, front_in[half, group, local], face, row)
            if half == 0:
                coupled()

        if half == 0:

            @pl.when(jnp.logical_not(upstream))
            def _():
                for local in range(GROUP):
                    res_ref[local] = rhs_row(group * GROUP + local).astype(BF16)

        else:
            coupled()

        for local in range(GROUP):
            row = group * GROUP + local
            lanes = slice(local * LANES, (local + 1) * LANES)
            residual = res_ref[local]
            kinds = kind_ref[pl.ds(row, 1), :]
            for kind in range(KD):
                masked = residual * jnp.where(kinds == kind, 1.0, 0.0).astype(BF16)
                rest = KD * WIDE + kind * (BLOCK - WIDE)
                inv_stack[kind * WIDE : (kind + 1) * WIDE, lanes] = masked[:WIDE]
                inv_stack[rest : rest + BLOCK - WIDE, lanes] = masked[WIDE:]
        updated = jnp.dot(inv_ref[...], inv_stack[...], preferred_element_type=F32)
        first = NP * NP * (NP - 1) if forward else 0
        for local in range(GROUP):
            value = updated[:, local * LANES : (local + 1) * LANES]
            for var in range(NVAR):
                start = var * NP * NP * NP + first
                front_out[half, group, local, var * NP * NP : (var + 1) * NP * NP, :] = value[
                    start : start + NP * NP, :
                ].astype(BF16)

        @pl.when(downstream)
        def _():
            front_copy(half, group, step).start()

        for local in range(GROUP):
            row = group * GROUP + local
            value = updated[:, local * LANES : (local + 1) * LANES]
            if half == HALVES - 1:
                out_ref[pl.ds(row, BLOCK, stride=rows), :] = value
            else:
                u_ref[row] = value
        if half == HALVES - 1:
            return
        for side in range(2):
            first_row = edge_y(group * GROUP, side)
            packed = turned(first_row, side)
            for local in range(1, GROUP):
                other = turned(edge_y(group * GROUP + local, side), local + side)
                packed = jnp.where(lane == local, other, packed)
            y_out[half, side, group] = packed.astype(BF16)

            @pl.when(has("cy", 2 * side - 1))
            def _():
                y_copy(half, side, group).start()

        for local in range(GROUP):
            row = group * GROUP + local
            x_low[half, row + 1] = edge_x(row, local, 0)
            x_high[half, row + 1] = edge_x(row, local, 1)
        for side in range(2):

            @pl.when(x_here(side, group))
            def _():
                x_copy(half, side).start()

    for half in range(HALVES):
        step = 1 if half % 2 == 0 else -1
        upstream = has("sweep", -step)
        downstream = has("sweep", step)

        @pl.when(upstream)
        def _():
            if half == 0:
                lay_out_coupling()
            else:

                @pl.loop(0, groups)
                def _(turn):
                    lateral(half - 1, place_of(turn))

        @pl.loop(0, groups)
        def _(turn):
            group = place_of(turn)
            if half > 0:

                @pl.when(jnp.logical_not(upstream))
                def _():
                    lateral(half - 1, group)

            update(half, group, upstream, downstream)

        if half == 0:

            @pl.when(jnp.logical_not(upstream))
            def _():
                lay_out_coupling()

    for half in range(HALVES):
        step = 1 if half % 2 == 0 else -1

        @pl.when(has("sweep", step))
        def _():
            @pl.loop(0, groups)
            def _(group):
                front_copy(half, group, step).wait_send()

        if half < HALVES - 1:
            for side in range(2):

                @pl.when(has("cy", 2 * side - 1))
                def _():
                    @pl.loop(0, groups)
                    def _(group):
                        y_copy(half, side, group).wait_send()

                @pl.when(has("cx", 2 * side - 1))
                def _():
                    x_copy(half, side).wait_send()


def shards(right_side, inverse_table, coupling_table, block_kind, face_kind):
    _, _, rows, width_y = right_side.shape
    groups = rows // GROUP
    columns = GROUP * LANES
    vmem = pl.BlockSpec(memory_space=pltpu.VMEM)
    hbm = pl.BlockSpec(memory_space=pltpu.HBM)
    inputs = KC * 6 * TRACE
    result = pl.pallas_call(
        functools.partial(kernel, rows),
        out_shape=jax.ShapeDtypeStruct((BLOCK * rows, LANES), F32),
        in_specs=[hbm] * 5,
        out_specs=vmem,
        scratch_shapes=[
            pltpu.VMEM((BLOCK * rows, LANES), F32),
            pltpu.VMEM((KD, BLOCK, BLOCK), BF16),
            pltpu.VMEM((inputs, BLOCK), BF16),
            pltpu.VMEM((rows, LANES), jnp.int32),
            pltpu.VMEM((6, rows, LANES), jnp.int32),
            pltpu.SemaphoreType.DMA((5,)),
            pltpu.VMEM((BLOCK, KD * BLOCK), BF16),
            pltpu.VMEM((8 * LANES, 3 * LANES), BF16),
            pltpu.VMEM((BLOCK, inputs), BF16),
            pltpu.VMEM((rows, BLOCK, LANES), F32),
            pltpu.VMEM((GROUP, BLOCK, LANES), BF16),
            pltpu.VMEM((GROUP, 2, TRACE, LANES), F32),
            pltpu.VMEM((groups, inputs, columns), BF16),
            pltpu.VMEM((KD * BLOCK, columns), BF16),
            pltpu.VMEM((HALVES, groups, GROUP, TRACE, LANES), BF16),
            pltpu.VMEM((HALVES, groups, GROUP, TRACE, LANES), BF16),
            pltpu.VMEM((HALVES - 1, rows + 2, TRACE, LANES), BF16),
            pltpu.VMEM((HALVES - 1, rows + 2, TRACE, LANES), BF16),
            pltpu.VMEM((HALVES - 1, 2, groups, TRACE, LANES), BF16),
            pltpu.VMEM((HALVES - 1, 2, groups, TRACE, LANES), BF16),
            pltpu.SemaphoreType.DMA((HALVES, groups)),
            pltpu.SemaphoreType.DMA((HALVES, groups)),
            pltpu.SemaphoreType.DMA((HALVES - 1, 2)),
            pltpu.SemaphoreType.DMA((HALVES - 1, 2)),
            pltpu.SemaphoreType.DMA((HALVES - 1, 2, groups)),
            pltpu.SemaphoreType.DMA((HALVES - 1, 2, groups)),
        ],
        compiler_params=pltpu.CompilerParams(
            collective_id=0, has_side_effects=True, vmem_limit_bytes=62 << 20
        ),
    )(
        right_side.reshape(BLOCK * rows, width_y),
        inverse_table,
        coupling_table.reshape(inputs, BLOCK),
        block_kind.reshape(rows, width_y),
        face_kind.reshape(6, rows, width_y),
    )
    return result.reshape(right_side.shape)


def solution(mesh):
    in_specs = (
        P("sweep", None, "cx", "cy"),
        P(),
        P(),
        P("sweep", "cx", "cy"),
        P("sweep", None, "cx", "cy"),
    )
    out_specs = P("sweep", None, "cx", "cy")
    return jax.shard_map(shards, mesh=mesh, in_specs=in_specs, out_specs=out_specs, check_vma=False)
```

```python
import functools
import jax
import jax.numpy as jnp
from jax import lax
from jax.experimental import pallas as pl
from jax.experimental.pallas import tpu as pltpu
from jax.sharding import PartitionSpec as P

NVAR = 5
NP = 4
BLOCK = 320
TRACE = 80
KD = 4
KC = 2
SWEEPS = 2
HALVES = 2 * SWEEPS
LANES = 128
WIDE = 256
DEPTH = 1024
GROUP = 2
MESH = pl.DeviceIdType.MESH
F32 = jnp.float32
BF16 = jnp.bfloat16


def kernel(
    rows,
    rhs_in,
    table_in,
    coupling_in,
    kind_in,
    face_in,
    out_ref,
    rhs_ref,
    table_ref,
    coupling_ref,
    kind_ref,
    face_ref,
    load_sem,
    inv_ref,
    tall_ref,
    wide_ref,
    u_ref,
    res_ref,
    tr_ref,
    stack,
    inv_stack,
    front_in,
    front_out,
    x_low,
    x_high,
    y_in,
    y_out,
    front_send,
    front_recv,
    x_send,
    x_recv,
    y_send,
    y_recv,
):
    groups = rows // GROUP
    loads = [
        pltpu.make_async_copy(source, target, load_sem.at[spot])
        for spot, (source, target) in enumerate(
            (
                (table_in, table_ref),
                (rhs_in, rhs_ref),
                (kind_in, kind_ref),
                (coupling_in, coupling_ref),
                (face_in, face_ref),
            )
        )
    ]
    for load in loads:
        load.start()
    places = {}
    for name in ("sweep", "cx", "cy"):
        places[name] = (lax.axis_index(name), lax.axis_size(name))

    def has(name, step):
        spot, count = places[name]
        return spot < count - 1 if step > 0 else spot > 0

    def partner(name, step):
        return {name: places[name][0] + step}

    for half in range(HALVES - 1):
        x_high[half, 0] = jnp.zeros((TRACE, LANES), BF16)
        x_low[half, rows + 1] = jnp.zeros((TRACE, LANES), BF16)
    for side in range(2):

        @pl.when(jnp.logical_not(has("cy", 2 * side - 1)))
        def _():
            for half in range(HALVES - 1):
                y_in[half, side] = jnp.zeros((groups, TRACE, LANES), BF16)

    barrier = pltpu.get_barrier_semaphore()
    total = 0
    for name in ("sweep", "cx", "cy"):
        for step in (-1, 1):
            exists = has(name, step)
            total = total + jnp.where(exists, 1, 0)

            @pl.when(exists)
            def _():
                pl.semaphore_signal(
                    barrier, inc=1, device_id=partner(name, step), device_id_type=MESH
                )

    stack[...] = jnp.zeros(stack.shape, BF16)
    loads[0].wait()
    for kind in range(KD):
        inv_ref[:, kind * WIDE : (kind + 1) * WIDE] = table_ref[kind, :, :WIDE]
    for pair in range(KD // 2):
        inv_ref[:, KD * WIDE + pair * LANES : KD * WIDE + (pair + 1) * LANES] = jnp.concatenate(
            [table_ref[2 * pair, :, WIDE:], table_ref[2 * pair + 1, :, WIDE:]], axis=1
        )
    for load in loads[1:]:
        load.wait()
    pl.semaphore_wait(barrier, total)

    def lay_out_coupling():
        filled = KC * 6 * TRACE
        tall_ref[:filled, :BLOCK] = coupling_ref[...]
        tall_ref[filled:, :BLOCK] = jnp.zeros((DEPTH - filled, BLOCK), BF16)
        wide_ref[...] = jnp.transpose(tall_ref[...])[:BLOCK]

    lane = lax.broadcasted_iota(jnp.int32, (TRACE, LANES), 1)
    flip = lax.rem(places["cx"][0], 2)

    def place_of(turn):
        return turn + flip * (groups - 1 - 2 * turn)

    def front_copy(half, group, step):
        return pltpu.make_async_remote_copy(
            src_ref=front_out.at[half, group],
            dst_ref=front_in.at[half, group],
            send_sem=front_send.at[half, group],
            recv_sem=front_recv.at[half, group],
            device_id=partner("sweep", step),
            device_id_type=MESH,
        )

    def x_copy(half, side):
        source, target = (x_low.at[half, 1], x_low.at[half, rows + 1])
        if side == 1:
            source, target = (x_high.at[half, rows], x_high.at[half, 0])
        return pltpu.make_async_remote_copy(
            src_ref=source,
            dst_ref=target,
            send_sem=x_send.at[half, side],
            recv_sem=x_recv.at[half, 1 - side],
            device_id=partner("cx", 2 * side - 1),
            device_id_type=MESH,
        )

    def y_copy(half, side, group):
        return pltpu.make_async_remote_copy(
            src_ref=y_out.at[half, side, group],
            dst_ref=y_in.at[half, 1 - side, group],
            send_sem=y_send.at[half, side, group],
            recv_sem=y_recv.at[half, 1 - side, group],
            device_id=partner("cy", 2 * side - 1),
            device_id_type=MESH,
        )

    def x_here(side, group):
        return jnp.logical_and(has("cx", 2 * side - 1), group == (groups - 1) * side)

    def rhs_row(row):
        return rhs_ref[pl.ds(row, BLOCK, stride=rows), :]

    def put_masked(group, lanes, value, face, row):
        one = face_ref[face, pl.ds(row, 1), :].astype(F32)
        place = face * TRACE
        stack[group, place : place + TRACE, lanes] = value * (1.0 - one).astype(BF16)
        place = (6 + face) * TRACE
        stack[group, place : place + TRACE, lanes] = value * one.astype(BF16)

    def edge_x(row, local, side):
        first = (NP - 1) * NP * side
        for node in range(NP):
            tr_ref[local, side, pl.ds(node, NVAR * NP, stride=NP), :] = u_ref[
                row, pl.ds(first + node, NVAR * NP, stride=NP * NP), :
            ]
        return tr_ref[local, side].astype(BF16)

    def edge_y(row, side):
        return u_ref[row, pl.ds((NP - 1) * side, TRACE, stride=NP), :]

    def turned(value, shift):
        return pltpu.roll(value, shift % LANES, 1) if shift % LANES else value

    def lateral(half, group):
        for side in range(2):

            @pl.when(x_here(side, group))
            def _():
                x_copy(half, 1 - side).wait_recv()

            @pl.when(has("cy", 2 * side - 1))
            def _():
                y_copy(half, 1 - side, group).wait_recv()

        for local in range(GROUP):
            row = group * GROUP + local
            lanes = slice(local * LANES, (local + 1) * LANES)
            put_masked(group, lanes, x_high[half, row], 2, row)
            put_masked(group, lanes, x_low[half, row + 2], 3, row)
            seen = turned(y_in[half, 0, group].astype(F32), -local)
            from_ylow = jnp.where(lane == 0, seen, turned(edge_y(row, 1), 1))
            put_masked(group, lanes, from_ylow.astype(BF16), 4, row)
            seen = turned(y_in[half, 1, group].astype(F32), -1 - local)
            from_yhigh = jnp.where(lane == LANES - 1, seen, turned(edge_y(row, 0), -1))
            put_masked(group, lanes, from_yhigh.astype(BF16), 5, row)

    def update(half, group, upstream, downstream):
        forward = half % 2 == 0
        step = 1 if forward else -1

        def coupled():
            product = jnp.dot(wide_ref[...], stack[group], preferred_element_type=F32)
            for local in range(GROUP):
                row = group * GROUP + local
                part = product[:, local * LANES : (local + 1) * LANES]
                res_ref[local] = (rhs_row(row) - part).astype(BF16)

        @pl.when(upstream)
        def _():
            front_copy(half, group, step).wait_recv()
            face = 0 if forward else 1
            for local in range(GROUP):
                row = group * GROUP + local
                lanes = slice(local * LANES, (local + 1) * LANES)
                put_masked(group, lanes, front_in[half, group, local], face, row)
            if half == 0:
                coupled()

        if half == 0:

            @pl.when(jnp.logical_not(upstream))
            def _():
                for local in range(GROUP):
                    res_ref[local] = rhs_row(group * GROUP + local).astype(BF16)

        else:
            coupled()

        for local in range(GROUP):
            row = group * GROUP + local
            lanes = slice(local * LANES, (local + 1) * LANES)
            residual = res_ref[local]
            kinds = kind_ref[pl.ds(row, 1), :]
            for kind in range(KD):
                masked = residual * jnp.where(kinds == kind, 1.0, 0.0).astype(BF16)
                rest = KD * WIDE + kind * (BLOCK - WIDE)
                inv_stack[kind * WIDE : (kind + 1) * WIDE, lanes] = masked[:WIDE]
                inv_stack[rest : rest + BLOCK - WIDE, lanes] = masked[WIDE:]
        updated = jnp.dot(inv_ref[...], inv_stack[...], preferred_element_type=F32)
        first = NP * NP * (NP - 1) if forward else 0
        for local in range(GROUP):
            value = updated[:, local * LANES : (local + 1) * LANES]
            for var in range(NVAR):
                start = var * NP * NP * NP + first
                front_out[half, group, local, var * NP * NP : (var + 1) * NP * NP, :] = value[
                    start : start + NP * NP, :
                ].astype(BF16)

        @pl.when(downstream)
        def _():
            front_copy(half, group, step).start()

        for local in range(GROUP):
            row = group * GROUP + local
            value = updated[:, local * LANES : (local + 1) * LANES]
            if half == HALVES - 1:
                out_ref[pl.ds(row, BLOCK, stride=rows), :] = value
            else:
                u_ref[row] = value
        if half == HALVES - 1:
            return
        for side in range(2):
            first_row = edge_y(group * GROUP, side)
            packed = turned(first_row, side)
            for local in range(1, GROUP):
                other = turned(edge_y(group * GROUP + local, side), local + side)
                packed = jnp.where(lane == local, other, packed)
            y_out[half, side, group] = packed.astype(BF16)

            @pl.when(has("cy", 2 * side - 1))
            def _():
                y_copy(half, side, group).start()

        for local in range(GROUP):
            row = group * GROUP + local
            x_low[half, row + 1] = edge_x(row, local, 0)
            x_high[half, row + 1] = edge_x(row, local, 1)
        for side in range(2):

            @pl.when(x_here(side, group))
            def _():
                x_copy(half, side).start()

    for half in range(HALVES):
        step = 1 if half % 2 == 0 else -1
        upstream = has("sweep", -step)
        downstream = has("sweep", step)

        @pl.when(upstream)
        def _():
            if half == 0:
                lay_out_coupling()
            else:

                @pl.loop(0, groups)
                def _(turn):
                    lateral(half - 1, place_of(turn))

        @pl.loop(0, groups)
        def _(turn):
            group = place_of(turn)
            if half > 0:

                @pl.when(jnp.logical_not(upstream))
                def _():
                    lateral(half - 1, group)

            update(half, group, upstream, downstream)

        if half == 0:

            @pl.when(jnp.logical_not(upstream))
            def _():
                lay_out_coupling()

    for half in range(HALVES):
        step = 1 if half % 2 == 0 else -1

        @pl.when(has("sweep", step))
        def _():
            @pl.loop(0, groups)
            def _(group):
                front_copy(half, group, step).wait_send()

        if half < HALVES - 1:
            for side in range(2):

                @pl.when(has("cy", 2 * side - 1))
                def _():
                    @pl.loop(0, groups)
                    def _(group):
                        y_copy(half, side, group).wait_send()

                @pl.when(has("cx", 2 * side - 1))
                def _():
                    x_copy(half, side).wait_send()


def shards(right_side, inverse_table, coupling_table, block_kind, face_kind):
    _, _, rows, width_y = right_side.shape
    groups = rows // GROUP
    columns = GROUP * LANES
    vmem = pl.BlockSpec(memory_space=pltpu.VMEM)
    hbm = pl.BlockSpec(memory_space=pltpu.HBM)
    inputs = KC * 6 * TRACE
    result = pl.pallas_call(
        functools.partial(kernel, rows),
        out_shape=jax.ShapeDtypeStruct((BLOCK * rows, LANES), F32),
        in_specs=[hbm] * 5,
        out_specs=vmem,
        scratch_shapes=[
            pltpu.VMEM((BLOCK * rows, LANES), F32),
            pltpu.VMEM((KD, BLOCK, BLOCK), BF16),
            pltpu.VMEM((inputs, BLOCK), BF16),
            pltpu.VMEM((rows, LANES), jnp.int32),
            pltpu.VMEM((6, rows, LANES), jnp.int32),
            pltpu.SemaphoreType.DMA((5,)),
            pltpu.VMEM((BLOCK, KD * BLOCK), BF16),
            pltpu.VMEM((DEPTH, 3 * LANES), BF16),
            pltpu.VMEM((BLOCK, DEPTH), BF16),
            pltpu.VMEM((rows, BLOCK, LANES), F32),
            pltpu.VMEM((GROUP, BLOCK, LANES), BF16),
            pltpu.VMEM((GROUP, 2, TRACE, LANES), F32),
            pltpu.VMEM((groups, DEPTH, columns), BF16),
            pltpu.VMEM((KD * BLOCK, columns), BF16),
            pltpu.VMEM((HALVES, groups, GROUP, TRACE, LANES), BF16),
            pltpu.VMEM((HALVES, groups, GROUP, TRACE, LANES), BF16),
            pltpu.VMEM((HALVES - 1, rows + 2, TRACE, LANES), BF16),
            pltpu.VMEM((HALVES - 1, rows + 2, TRACE, LANES), BF16),
            pltpu.VMEM((HALVES - 1, 2, groups, TRACE, LANES), BF16),
            pltpu.VMEM((HALVES - 1, 2, groups, TRACE, LANES), BF16),
            pltpu.SemaphoreType.DMA((HALVES, groups)),
            pltpu.SemaphoreType.DMA((HALVES, groups)),
            pltpu.SemaphoreType.DMA((HALVES - 1, 2)),
            pltpu.SemaphoreType.DMA((HALVES - 1, 2)),
            pltpu.SemaphoreType.DMA((HALVES - 1, 2, groups)),
            pltpu.SemaphoreType.DMA((HALVES - 1, 2, groups)),
        ],
        compiler_params=pltpu.CompilerParams(
            collective_id=0, has_side_effects=True, vmem_limit_bytes=62 << 20
        ),
    )(
        right_side.reshape(BLOCK * rows, width_y),
        inverse_table,
        coupling_table.reshape(inputs, BLOCK),
        block_kind.reshape(rows, width_y),
        face_kind.reshape(6, rows, width_y),
    )
    return result.reshape(right_side.shape)


def solution(mesh):
    in_specs = (
        P("sweep", None, "cx", "cy"),
        P(),
        P(),
        P("sweep", "cx", "cy"),
        P("sweep", None, "cx", "cy"),
    )
    out_specs = P("sweep", None, "cx", "cy")
    return jax.shard_map(shards, mesh=mesh, in_specs=in_specs, out_specs=out_specs, check_vma=False)
```
